32 devices in a mesh: rows: 16 (over z, y, x), width: 2 (over core).
Axes of the slice: x: 2, y: 2, z: 4, core: 2. Of those that a mesh axis runs over, the one named last changes fastest.
Arguments:
- left_feat: bfloat16 [16, 2048, 256], P('rows', 'width'), may hold values from -28 to 28
- right_feat: bfloat16 [16, 2048, 256], P('rows', 'width'), may hold values from -28 to 28
- refine_weight: bfloat16 [3, 3, 256, 256], replicated, may hold values from -0.125 to 0.125
Outputs:
- disparity: float32 [16, 2048], P('rows', 'width')
- refined: bfloat16 [16, 2048, 256], P('rows', 'width')
The draws below stay inside these ranges and needn't reach their ends.
All inputs are finite; a program needn't handle non-finite values.
Results may differ from the reference program's by a relative error of at most 0.0049.
Values may be sent and summed in bfloat16 or wider, within the bound.
A program may use at most 64 MiB of HBM per device.

```python
import math
import jax
import jax.numpy as jnp
from jax import lax

C = 256
W_DEV = 1024
ROWS = 16
W = 2048


def feature_pair(key):
    base = jax.random.fold_in(key, 911)
    key_right, key_noise, key_match = jax.random.split(base, 3)
    col_positions = jnp.arange(W, dtype=jnp.int32)
    shape = (ROWS, W, C)
    right_values = jax.random.truncated_normal(key_right, -4.0, 4.0, shape, jnp.float32)
    noise_values = jax.random.truncated_normal(key_noise, -4.0, 4.0, shape, jnp.float32)
    match_cols = jax.random.randint(key_match, (ROWS, W), 0, col_positions[None, :] + 1)
    gathered = jnp.take_along_axis(right_values, match_cols[:, :, None], axis=1)
    left_values = 0.7 * gathered + 0.7 * noise_values
    return (left_values.astype(jnp.bfloat16), right_values.astype(jnp.bfloat16))


def draw_left_feat(key, part):
    return feature_pair(key)[0]


def draw_right_feat(key, part):
    return feature_pair(key)[1]


def gaussian(own_key, dims, spread, most, kind=jnp.bfloat16):
    values = spread * jax.random.normal(own_key, dims, jnp.float32)
    return jnp.clip(values, min=-most, max=most).astype(kind)


def setup_inputs(seed: int = 0) -> dict:
    splits = jax.random.split(jax.random.key(seed), 4)
    left_feat = draw_left_feat(jax.random.fold_in(splits[3], 71), 0)
    right_feat = draw_right_feat(jax.random.fold_in(splits[3], 71), 0)
    refine_weight = gaussian(splits[2], (3, 3, C, C), (9 * C) ** -0.5, 0.125)
    return {"left_feat": left_feat, "right_feat": right_feat, "refine_weight": refine_weight}


NEG_FILL = -1e+30

def reference(left_feat, right_feat, refine_weight):
    n_rows, n_cols, chans = left_feat.shape
    score_scale = 1.0 / math.sqrt(chans)
    col_positions = jnp.arange(n_cols, dtype=jnp.int32)
    n_blocks = n_cols // W_DEV

    def one_block(index_pair):
        row_index, blk_index = index_pair
        queries = lax.dynamic_slice(left_feat, (row_index.astype(jnp.int32), (blk_index * W_DEV).astype(jnp.int32), jnp.int32(0)), (1, W_DEV, chans))[0]
        keys_row = lax.dynamic_index_in_dim(right_feat, row_index.astype(jnp.int32), 0, keepdims=False)
        query_positions = blk_index * W_DEV + jnp.arange(W_DEV, dtype=jnp.int32)
        scores = jnp.dot(queries, keys_row.T, preferred_element_type=jnp.float32) * score_scale
        allowed = col_positions[None, :] <= query_positions[:, None]
        scores = jnp.where(allowed, scores, NEG_FILL)
        row_max = scores.max(-1)
        weights = jnp.where(allowed, jnp.exp(scores - row_max[:, None]), 0.0)
        denominator = weights.sum(-1)
        matched = (jnp.dot(weights.astype(jnp.bfloat16), keys_row, preferred_element_type=jnp.float32) / denominator[:, None]).astype(jnp.bfloat16)
        expected = (weights * col_positions.astype(jnp.float32)[None, :]).sum(-1) / denominator
        return (matched, query_positions.astype(jnp.float32) - expected)
    row_ids = jnp.repeat(jnp.arange(n_rows, dtype=jnp.int32), n_blocks)
    blk_ids = jnp.tile(jnp.arange(n_blocks, dtype=jnp.int32), n_rows)
    matched, disparity = lax.map(one_block, (row_ids, blk_ids))
    matched = matched.reshape(n_rows, n_cols, chans)
    disparity = disparity.reshape(n_rows, n_cols)
    padded = jnp.pad(matched, ((1, 1), (1, 1), (0, 0)))
    total = jnp.zeros((n_rows * n_cols, chans), jnp.float32)
    for tap_row in range(3):
        for tap_col in range(3):
            window = padded[tap_row:tap_row + n_rows, tap_col:tap_col + n_cols].reshape(-1, chans)
            total = total + jnp.dot(window, refine_weight[tap_row, tap_col], preferred_element_type=jnp.float32)
    refined = total.reshape(n_rows, n_cols, chans).astype(jnp.bfloat16)
    return (disparity, refined)
```

```python
import functools
import math

import jax
import jax.numpy as jnp
from jax import lax
from jax.experimental import pallas as pl
from jax.experimental.pallas import tpu as pltpu
from jax.sharding import PartitionSpec as P

NEG_FILL = -1e30


def extended(value, sides, width):
    for axis, dim in sides:
        size, length = (lax.axis_size(axis), value.shape[dim])
        up = [(i, (i + 1) % size) for i in range(size - 1)]
        down = [(j, i) for i, j in up]
        last = lax.slice_in_dim(value, length - width, length, axis=dim)
        leading = lax.slice_in_dim(value, 0, width, axis=dim)
        before = lax.ppermute(last, axis, up)
        after = lax.ppermute(leading, axis, down)
        value = jnp.concatenate([before, value, after], axis=dim)
    return value


def absorb_block(state_now, query_rows, query_positions, sub_keys, key_positions):
    run_max, run_total, weighted, position_sum = state_now
    score_scale = 1.0 / math.sqrt(query_rows.shape[-1])
    scores = (
        jnp.einsum("rqc,rkc->rqk", query_rows, sub_keys, preferred_element_type=jnp.float32)
        * score_scale
    )
    allowed = (key_positions[None, :] <= query_positions[:, None]) & (key_positions[None, :] >= 0)
    scores = jnp.where(allowed[None], scores, NEG_FILL)
    new_max = jnp.maximum(run_max, scores.max(-1))
    factor = jnp.exp(run_max - new_max)
    weights = jnp.where(allowed[None], jnp.exp(scores - new_max[..., None]), 0.0)
    run_total = run_total * factor + weights.sum(-1)
    weighted = weighted * factor[..., None] + jnp.einsum(
        "rqk,rkc->rqc", weights.astype(jnp.bfloat16), sub_keys, preferred_element_type=jnp.float32
    )
    position_sum = position_sum * factor + (
        weights * key_positions.astype(jnp.float32)[None, None, :]
    ).sum(-1)
    return (new_max, run_total, weighted, position_sum)


def absorb_piece(state_now, query_rows, query_positions, key_piece):
    n_keys = key_piece.shape[1]
    sub_len = math.gcd(n_keys, 512)
    count = n_keys // sub_len
    last_query = query_positions[-1]

    def one_sub(carry_state, sub_index):
        sub_start = sub_index * sub_len
        sub_keys = lax.dynamic_slice_in_dim(key_piece, sub_index * sub_len, sub_len, 1)
        key_positions = sub_start + jnp.arange(sub_len, dtype=jnp.int32)
        result_state = lax.cond(
            sub_start <= last_query,
            lambda inner: absorb_block(inner, query_rows, query_positions, sub_keys, key_positions),
            lambda inner: inner,
            carry_state,
        )
        return (result_state, None)

    result, _ = lax.scan(one_sub, state_now, jnp.arange(count, dtype=jnp.int32))
    return result


def empty_state(rows_here, length, chans):
    return (
        jnp.full((rows_here, length), NEG_FILL, jnp.float32),
        jnp.zeros((rows_here, length), jnp.float32),
        jnp.zeros((rows_here, length, chans), jnp.float32),
        jnp.zeros((rows_here, length), jnp.float32),
    )


def finish_state(state_now, query_positions):
    run_max, run_total, weighted, position_sum = state_now
    matched = (weighted / run_total[..., None]).astype(jnp.bfloat16)
    disparity = query_positions.astype(jnp.float32)[None, :] - position_sum / run_total
    return (matched, disparity)


def body(left_feat, right_feat, refine_weight):
    rows_here, block_len, chans = left_feat.shape
    my_index = lax.axis_index("width")
    offset = my_index * block_len
    query_positions = offset + jnp.arange(block_len, dtype=jnp.int32)
    final_state = absorb_piece(
        empty_state(rows_here, block_len, chans),
        left_feat,
        query_positions,
        lax.all_gather(right_feat, "width", axis=1, tiled=True),
    )
    matched, disparity = finish_state(final_state, query_positions)
    padded = extended(matched, (("rows", 0), ("width", 1)), 1)
    total = jnp.zeros((rows_here * block_len, chans), jnp.float32)
    for tap_row in range(3):
        for tap_col in range(3):
            window = padded[tap_row : tap_row + rows_here, tap_col : tap_col + block_len].reshape(
                -1, chans
            )
            total = total + jnp.dot(
                window, refine_weight[tap_row, tap_col], preferred_element_type=jnp.float32
            )
    refined = total.reshape(rows_here, block_len, chans).astype(jnp.bfloat16)
    return (disparity, refined)


MESH = pl.DeviceIdType.MESH
EDGE = 16
LANES = 128
CHUNK = 128
VMEM_LIMIT = 32 * 1024 * 1024


def attend(left, keys, scores, own, disp_ref, tile, first_key_tile, size):
    chans = left.shape[-1]
    gain = math.log2(math.e) / math.sqrt(chans)
    n_tiles = first_key_tile + tile + 1
    rows = pl.ds(tile * size, size)
    queries = left[rows, :]
    lane_max = jnp.full((size, LANES), NEG_FILL, jnp.float32)
    for kt in range(n_tiles):
        s = lax.dot_general(
            queries,
            keys[pl.ds(kt * size, size), :],
            (((1,), (1,)), ((), ())),
            preferred_element_type=jnp.float32,
        )
        if kt == n_tiles - 1:
            q_at = lax.broadcasted_iota(jnp.int32, (size, size), 0)
            k_at = lax.broadcasted_iota(jnp.int32, (size, size), 1)
            s = jnp.where(k_at <= q_at, s, NEG_FILL)
        scores[:, pl.ds(kt * size, size)] = s
        for c in range(0, size, LANES):
            lane_max = jnp.maximum(lane_max, s[:, c : c + LANES])
    row_max = jnp.max(lane_max, axis=1, keepdims=True)
    total = jnp.zeros((size, LANES), jnp.float32)
    prefix = jnp.zeros((size, LANES), jnp.float32)
    acc = jnp.zeros((size, chans), jnp.float32)
    for kt in range(n_tiles):
        p = jnp.exp2((scores[:, pl.ds(kt * size, size)] - row_max) * gain)
        for c in range(0, size, LANES):
            total = total + p[:, c : c + LANES]
            prefix = prefix + total
        acc = acc + jnp.dot(
            p.astype(jnp.bfloat16),
            keys[pl.ds(kt * size, size), :],
            preferred_element_type=jnp.float32,
        )
    denominator = jnp.sum(total, axis=1, keepdims=True)
    own[rows, :] = (acc * (1.0 / denominator)).astype(jnp.bfloat16)
    n_chunks = n_tiles * (size // LANES)
    lane = lax.broadcasted_iota(jnp.int32, (size, LANES), 1).astype(jnp.float32)
    position = LANES * (n_chunks * total - prefix) + lane * total
    total_t = jnp.sum(total.T, axis=0, keepdims=True)
    position_t = jnp.sum(position.T, axis=0, keepdims=True)
    at = lax.broadcasted_iota(jnp.int32, (1, size), 1) + (n_tiles - 1) * size
    disp_ref[:, rows] = at.astype(jnp.float32) - position_t / total_t


def kernel(
    n_rows, size, chunk,
    left_hbm, right_hbm, weight_hbm,
    disp_ref, out_ref,
    left, keys, weight, scores, own, near, far, made, given, edges, sums, parts,
    load_sem, send_sem, key_sem, raw_x_sem, raw_y_sem, far_sem, given_sem, edge_sem,
):
    length, chans = left.shape
    half = length // 2
    n_tiles, n_chunks = length // size, half // chunk
    bf16 = jnp.bfloat16
    r, w = lax.axis_index("rows"), lax.axis_index("width")
    odd = r % 2
    other_w = 1 - w
    x_row = r + 1 - 2 * odd
    x_tap, far_tap = 2 - 2 * odd, 2 * odd
    below, above = r >= 2, r + 2 < n_rows
    ahead, behind = r - 2 + 4 * odd, r + 2 - 4 * odd
    to_ahead = ((odd == 1) & above) | ((odd == 0) & below)
    to_behind = ((odd == 1) & below) | ((odd == 0) & above)

    load_left = pltpu.make_async_copy(left_hbm.at[0], left, load_sem.at[0])
    load_right = pltpu.make_async_copy(
        right_hbm.at[0], keys.at[pl.ds(w * length, length)], load_sem.at[1]
    )
    load_weight = pltpu.make_async_copy(weight_hbm, weight, load_sem.at[2])
    load_left.start()
    load_right.start()
    load_weight.start()

    barrier = pltpu.get_barrier_semaphore()
    for there in ((r, other_w), (x_row, w)):
        pl.semaphore_signal(barrier, inc=1, device_id=there, device_id_type=MESH)

    @pl.when(below)
    def _():
        pl.semaphore_signal(barrier, inc=1, device_id=(r - 2, w), device_id_type=MESH)

    @pl.when(above)
    def _():
        pl.semaphore_signal(barrier, inc=1, device_id=(r + 2, w), device_id_type=MESH)

    def all_in():
        pl.semaphore_wait(barrier, 2 + below.astype(jnp.int32) + above.astype(jnp.int32))

    def remote(src, dst, sent, received, row, col):
        return pltpu.make_async_remote_copy(
            src_ref=src, dst_ref=dst, send_sem=send_sem.at[sent], recv_sem=received,
            device_id=(row, col), device_id_type=MESH,
        )

    def at16(start, n):
        return pl.ds(pl.multiple_of(start, EDGE), n)

    outer, inner = w * half, (1 - w) * half
    edge_at = (1 - w) * (length - EDGE)

    def part(base, k):
        return at16(base + k * chunk, chunk)

    def raw_x(k):
        here = part(outer, k)
        return remote(own.at[here], near.at[here], 1, raw_x_sem.at[k], x_row, w)

    def raw_y(k):
        here = part(inner, k)
        return remote(own.at[here], near.at[here], 2, raw_y_sem.at[k], ahead, w)

    def hand(k):
        here = part(outer, k)
        return remote(near.at[here], far.at[here], 3, far_sem.at[k], behind, w)

    def sum_copy(here, k):
        return remote(made.at[here], given.at[here], 4, given_sem.at[k], x_row, w)

    def edge_copy(j):
        src = own if j == 0 else near
        return remote(
            src.at[at16(edge_at, EDGE)], edges.at[j], 5, edge_sem.at[j], r, other_w
        )

    def span(base, k):
        if isinstance(k, int) and k == 0:
            return base + EDGE, chunk - 2 * EDGE
        return base + k * chunk - EDGE, chunk

    side_at = half - EDGE
    key_copy = remote(
        keys.at[pl.ds(0, length)], keys.at[pl.ds(0, length)], 0, key_sem.at[0], r, other_w
    )

    def dots(value, tap):
        return [
            jnp.dot(value, weight[tap, b], preferred_element_type=jnp.float32) for b in range(3)
        ]

    def put(ref, base, k, values):
        for b in range(3):
            ref[b, at16(EDGE + base + k * chunk, chunk), :] = values[b]

    def add(ref, base, k, values):
        for b in range(3):
            here = at16(EDGE + base + k * chunk, chunk)
            ref[b, here, :] = ref[b, here, :] + values[b]

    def shifted(ref, start, n):
        before = ref[0, pl.ds(pl.multiple_of(start + EDGE - 8, 8), n + 8), :]
        after = ref[2, at16(start + EDGE, n + 8), :]
        return (
            pltpu.roll(before, 1, 0)[8:, :]
            + ref[1, at16(start + EDGE, n), :]
            + pltpu.roll(after, n + 7, 0)[:n, :]
        )

    def emit(start, n, with_given):
        here = at16(start, n)
        total = shifted(sums, start, n)
        if with_given:
            total = total + given[here, :].astype(jnp.float32)
        out_ref[0, here, :] = total.astype(bf16)

    def give(start, n, k):
        here = at16(start, n)
        made[here, :] = shifted(parts, start, n).astype(bf16)
        sum_copy(here, k).start()

    def loop(body):
        body(0)
        lax.fori_loop(1, n_chunks, lambda k, _: (body(k), 0)[1], 0)

    def prepare(k, _):
        put(sums, outer, k, dots(own[part(outer, k), :], 1))
        value = own[part(inner, k), :]
        put(sums, inner, k, dots(value, 1))
        put(parts, inner, k, dots(value, far_tap))
        return 0

    def take_x(k):
        raw_x(k).wait_recv()

        @pl.when(to_behind)
        def _():
            hand(k).start()

        add(sums, outer, k, dots(near[part(outer, k), :], x_tap))

    def take_y(k):
        @pl.when(to_behind)
        def _():
            raw_y(k).wait_recv()

            @pl.when(k == (1 - w) * (n_chunks - 1))
            def _():
                edge_copy(1).start()

            add(parts, inner, k, dots(near[part(inner, k), :], x_tap))

        give(*span(inner, k), k)

    def take_far(k):
        @pl.when(to_ahead)
        def _():
            hand(k).wait_recv()
            add(sums, outer, k, dots(far[part(outer, k), :], far_tap))

        emit(*span(outer, k), False)

    def take_given(k):
        start, n = span(inner, k)
        sum_copy(at16(start, n), k).wait_recv()
        emit(start, n, True)

    def clear():
        zeros = jnp.zeros((EDGE, chans), jnp.float32)
        sums[0, pl.ds(0, EDGE), :] = zeros
        sums[2, pl.ds(EDGE + length, EDGE), :] = zeros
        for b in range(3):
            for k in range(2):
                parts[b, at16(EDGE + half - (2 - k) * EDGE + 2 * w * EDGE, EDGE), :] = zeros

    def rim():
        edge_copy(0).wait_recv()
        tap_col = 2 - 2 * w
        ours = jnp.dot(edges[0], weight[1, tap_col], preferred_element_type=jnp.float32)
        theirs = jnp.dot(edges[0], weight[far_tap, tap_col], preferred_element_type=jnp.float32)
        here = at16(other_w * (EDGE + length), EDGE)
        sums[tap_col, here, :] = ours
        parts[tap_col, here, :] = theirs

        @pl.when(to_behind)
        def _():
            edge_copy(1).wait_recv()
            parts[tap_col, here, :] = theirs + jnp.dot(
                edges[1], weight[x_tap, tap_col], preferred_element_type=jnp.float32
            )

        give(side_at, 2 * EDGE, n_chunks)
        give(edge_at, EDGE, n_chunks + 1)

    @pl.when(w == 0)
    def _():
        load_left.wait()
        load_right.wait()
        for tile in range(n_tiles):
            attend(left, keys, scores, own, disp_ref, tile, 0, size)
        all_in()
        key_copy.start()
        edge_copy(0).start()
        for k in range(n_chunks):
            raw_x(k).start()

            @pl.when(to_ahead)
            def _():
                raw_y(k).start()

        load_weight.wait()
        clear()
        lax.fori_loop(0, n_chunks, prepare, 0)

        def both(k):
            take_x(k)
            take_y(k)

        loop(both)

    @pl.when(w == 1)
    def _():
        load_left.wait()
        load_right.wait()
        load_weight.wait()
        clear()
        all_in()
        key_copy.wait_recv()
        per_tile = size // chunk
        for tile in range(n_tiles):
            attend(left, keys, scores, own, disp_ref, tile, n_tiles, size)
            if tile == 0:
                edge_copy(0).start()
            for k in range(tile * per_tile, (tile + 1) * per_tile):
                if k < n_chunks:

                    @pl.when(to_ahead)
                    def _():
                        raw_y(k).start()

                else:
                    raw_x(k - n_chunks).start()
        lax.fori_loop(0, n_chunks, prepare, 0)
        loop(take_y)
        loop(take_x)

    rim()

    def last(k):
        take_far(k)
        take_given(k)

    loop(last)
    sum_copy(at16(edge_at, EDGE), n_chunks + 1).wait_recv()
    emit(w * (length - EDGE), EDGE, False)
    emit(edge_at, EDGE, True)
    sum_copy(at16(side_at, 2 * EDGE), n_chunks).wait_recv()
    emit(side_at, 2 * EDGE, True)

    def sent(ref, n, which):
        remote(ref.at[pl.ds(0, n)], ref.at[pl.ds(0, n)], which, key_sem.at[0], x_row, w).wait_send()

    @pl.when(w == 0)
    def _():
        key_copy.wait_send()

    sent(own, half, 1)
    sent(made, half + EDGE, 4)
    sent(edges, 1, 5)

    @pl.when(to_ahead)
    def _():
        sent(own, half, 2)

    @pl.when(to_behind)
    def _():
        sent(near, half, 3)
        sent(edges, 1, 5)


def hand_on(disp_in, out_in, disp_ref, out_ref, sem):
    copies = [
        pltpu.make_async_copy(out_in, out_ref, sem.at[0]),
        pltpu.make_async_copy(disp_in, disp_ref, sem.at[1]),
    ]
    for copy in copies:
        copy.start()
    for copy in copies:
        copy.wait()


def fused(n_rows, left_feat, right_feat, refine_weight):
    _, length, chans = left_feat.shape
    half = length // 2
    size = math.gcd(half, 256)
    chunk = math.gcd(size, CHUNK)
    n_chunks = half // chunk
    bf16, f32 = jnp.bfloat16, jnp.float32
    dma = pltpu.SemaphoreType.DMA
    rows = pltpu.VMEM((length, chans), bf16)
    found = pl.pallas_call(
        functools.partial(kernel, n_rows, size, chunk),
        out_shape=(pltpu.VMEM((1, length), f32), pltpu.VMEM((1, length, chans), bf16)),
        in_specs=[pl.BlockSpec(memory_space=pltpu.HBM)] * 3,
        out_specs=[pl.BlockSpec(memory_space=pltpu.VMEM)] * 2,
        scratch_shapes=[
            rows,
            pltpu.VMEM((2 * length, chans), bf16),
            pltpu.VMEM((3, 3, chans, chans), bf16),
            pltpu.VMEM((size, 2 * length), f32),
            rows,
            rows,
            rows,
            rows,
            rows,
            pltpu.VMEM((2, EDGE, chans), bf16),
            pltpu.VMEM((3, length + 2 * EDGE, chans), f32),
            pltpu.VMEM((3, length + 2 * EDGE, chans), f32),
            dma((3,)),
            dma((6,)),
            dma((1,)),
            dma((n_chunks,)),
            dma((n_chunks,)),
            dma((n_chunks,)),
            dma((n_chunks + 2,)),
            dma((2,)),
        ],
        compiler_params=pltpu.CompilerParams(
            collective_id=0, has_side_effects=True, vmem_limit_bytes=VMEM_LIMIT
        ),
    )(*(pltpu.with_memory_space_constraint(x, pltpu.HBM) for x in (left_feat, right_feat, refine_weight)))
    return pl.pallas_call(
        hand_on,
        out_shape=(
            jax.ShapeDtypeStruct((1, length), f32),
            jax.ShapeDtypeStruct((1, length, chans), bf16),
        ),
        in_specs=[pl.BlockSpec(memory_space=pltpu.VMEM)] * 2,
        out_specs=[pl.BlockSpec(memory_space=pltpu.HBM)] * 2,
        scratch_shapes=[dma((2,))],
        compiler_params=pltpu.CompilerParams(vmem_limit_bytes=VMEM_LIMIT),
    )(*found)


def solution(mesh):
    n_rows, n_width = mesh.shape["rows"], mesh.shape["width"]

    def local(left_feat, right_feat, refine_weight):
        rows_here, length, chans = left_feat.shape
        fits = n_rows % 2 == 0 and n_width == 2 and rows_here == 1
        if fits and length % (2 * CHUNK) == 0 and chans % LANES == 0:
            return fused(n_rows, left_feat, right_feat, refine_weight)
        return body(left_feat, right_feat, refine_weight)

    placed = (P("rows", "width", None), P("rows", "width", None), P())
    return jax.shard_map(
        local,
        mesh=mesh,
        in_specs=placed,
        out_specs=(P("rows", "width"), P("rows", "width", None)),
        check_vma=False,
    )
```

```python
import functools
import math

import jax
import jax.numpy as jnp
from jax import lax
from jax.experimental import pallas as pl
from jax.experimental.pallas import tpu as pltpu
from jax.sharding import PartitionSpec as P

NEG_FILL = -1e30


def extended(value, sides, width):
    for axis, dim in sides:
        size, length = (lax.axis_size(axis), value.shape[dim])
        up = [(i, (i + 1) % size) for i in range(size - 1)]
        down = [(j, i) for i, j in up]
        last = lax.slice_in_dim(value, length - width, length, axis=dim)
        leading = lax.slice_in_dim(value, 0, width, axis=dim)
        before = lax.ppermute(last, axis, up)
        after = lax.ppermute(leading, axis, down)
        value = jnp.concatenate([before, value, after], axis=dim)
    return value


def absorb_block(state_now, query_rows, query_positions, sub_keys, key_positions):
    run_max, run_total, weighted, position_sum = state_now
    score_scale = 1.0 / math.sqrt(query_rows.shape[-1])
    scores = (
        jnp.einsum("rqc,rkc->rqk", query_rows, sub_keys, preferred_element_type=jnp.float32)
        * score_scale
    )
    allowed = (key_positions[None, :] <= query_positions[:, None]) & (key_positions[None, :] >= 0)
    scores = jnp.where(allowed[None], scores, NEG_FILL)
    new_max = jnp.maximum(run_max, scores.max(-1))
    factor = jnp.exp(run_max - new_max)
    weights = jnp.where(allowed[None], jnp.exp(scores - new_max[..., None]), 0.0)
    run_total = run_total * factor + weights.sum(-1)
    weighted = weighted * factor[..., None] + jnp.einsum(
        "rqk,rkc->rqc", weights.astype(jnp.bfloat16), sub_keys, preferred_element_type=jnp.float32
    )
    position_sum = position_sum * factor + (
        weights * key_positions.astype(jnp.float32)[None, None, :]
    ).sum(-1)
    return (new_max, run_total, weighted, position_sum)


def absorb_piece(state_now, query_rows, query_positions, key_piece):
    n_keys = key_piece.shape[1]
    sub_len = math.gcd(n_keys, 512)
    count = n_keys // sub_len
    last_query = query_positions[-1]

    def one_sub(carry_state, sub_index):
        sub_start = sub_index * sub_len
        sub_keys = lax.dynamic_slice_in_dim(key_piece, sub_index * sub_len, sub_len, 1)
        key_positions = sub_start + jnp.arange(sub_len, dtype=jnp.int32)
        result_state = lax.cond(
            sub_start <= last_query,
            lambda inner: absorb_block(inner, query_rows, query_positions, sub_keys, key_positions),
            lambda inner: inner,
            carry_state,
        )
        return (result_state, None)

    result, _ = lax.scan(one_sub, state_now, jnp.arange(count, dtype=jnp.int32))
    return result


def empty_state(rows_here, length, chans):
    return (
        jnp.full((rows_here, length), NEG_FILL, jnp.float32),
        jnp.zeros((rows_here, length), jnp.float32),
        jnp.zeros((rows_here, length, chans), jnp.float32),
        jnp.zeros((rows_here, length), jnp.float32),
    )


def finish_state(state_now, query_positions):
    run_max, run_total, weighted, position_sum = state_now
    matched = (weighted / run_total[..., None]).astype(jnp.bfloat16)
    disparity = query_positions.astype(jnp.float32)[None, :] - position_sum / run_total
    return (matched, disparity)


def body(left_feat, right_feat, refine_weight):
    rows_here, block_len, chans = left_feat.shape
    my_index = lax.axis_index("width")
    offset = my_index * block_len
    query_positions = offset + jnp.arange(block_len, dtype=jnp.int32)
    final_state = absorb_piece(
        empty_state(rows_here, block_len, chans),
        left_feat,
        query_positions,
        lax.all_gather(right_feat, "width", axis=1, tiled=True),
    )
    matched, disparity = finish_state(final_state, query_positions)
    padded = extended(matched, (("rows", 0), ("width", 1)), 1)
    total = jnp.zeros((rows_here * block_len, chans), jnp.float32)
    for tap_row in range(3):
        for tap_col in range(3):
            window = padded[tap_row : tap_row + rows_here, tap_col : tap_col + block_len].reshape(
                -1, chans
            )
            total = total + jnp.dot(
                window, refine_weight[tap_row, tap_col], preferred_element_type=jnp.float32
            )
    refined = total.reshape(rows_here, block_len, chans).astype(jnp.bfloat16)
    return (disparity, refined)


MESH = pl.DeviceIdType.MESH
EDGE = 16
LANES = 128
CHUNK = 128
VMEM_LIMIT = 32 * 1024 * 1024


def scan_keys(left, keys, scores, tile, first, n_tiles, masked, size):
    chans = left.shape[-1]
    gain = math.log2(math.e) / math.sqrt(chans)
    queries = left[pl.ds(tile * size, size), :]
    lane_max = jnp.full((size, LANES), NEG_FILL, jnp.float32)
    for kt in range(n_tiles):
        s = lax.dot_general(
            queries,
            keys[pl.ds((first + kt) * size, size), :],
            (((1,), (1,)), ((), ())),
            preferred_element_type=jnp.float32,
        )
        if masked and kt == n_tiles - 1:
            q_at = lax.broadcasted_iota(jnp.int32, (size, size), 0)
            k_at = lax.broadcasted_iota(jnp.int32, (size, size), 1)
            s = jnp.where(k_at <= q_at, s, NEG_FILL)
        scores[:, pl.ds(kt * size, size)] = s
        for c in range(0, size, LANES):
            lane_max = jnp.maximum(lane_max, s[:, c : c + LANES])
    row_max = jnp.max(lane_max, axis=1, keepdims=True)
    total = jnp.zeros((size, LANES), jnp.float32)
    prefix = jnp.zeros((size, LANES), jnp.float32)
    acc = jnp.zeros((size, chans), jnp.float32)
    for kt in range(n_tiles):
        p = jnp.exp2((scores[:, pl.ds(kt * size, size)] - row_max) * gain)
        for c in range(0, size, LANES):
            total = total + p[:, c : c + LANES]
            prefix = prefix + total
        acc = acc + jnp.dot(
            p.astype(jnp.bfloat16),
            keys[pl.ds((first + kt) * size, size), :],
            preferred_element_type=jnp.float32,
        )
    n_chunks = n_tiles * (size // LANES)
    lane = lax.broadcasted_iota(jnp.int32, (size, LANES), 1).astype(jnp.float32)
    position = LANES * (n_chunks * total - prefix) + (lane + first * size) * total
    return row_max, total, position, acc


def finish_tile(total, position, acc, own, disp_ref, tile, first_query_tile, size):
    rows = pl.ds(tile * size, size)
    denominator = jnp.sum(total, axis=1, keepdims=True)
    own[rows, :] = (acc * (1.0 / denominator)).astype(jnp.bfloat16)
    total_t = jnp.sum(total.T, axis=0, keepdims=True)
    position_t = jnp.sum(position.T, axis=0, keepdims=True)
    at = lax.broadcasted_iota(jnp.int32, (1, size), 1) + (first_query_tile + tile) * size
    disp_ref[:, rows] = at.astype(jnp.float32) - position_t / total_t


def attend_all(left, keys, scores, own, disp_ref, tile, size):
    _, *found = scan_keys(left, keys, scores, tile, 0, tile + 1, True, size)
    finish_tile(*found, own, disp_ref, tile, 0, size)


def attend_own(left, keys, scores, held, tile, n_tiles, size):
    rows = pl.ds(tile * size, size)
    held_max, held_total, held_position, held_acc = held
    row_max, total, position, acc = scan_keys(
        left, keys, scores, tile, n_tiles, tile + 1, True, size
    )
    held_max[rows, :] = jnp.broadcast_to(row_max, total.shape)
    held_total[rows, :] = total
    held_position[rows, :] = position
    held_acc[rows, :] = acc


def attend_rest(left, keys, scores, held, own, disp_ref, tile, n_tiles, size):
    gain = math.log2(math.e) / math.sqrt(left.shape[-1])
    rows = pl.ds(tile * size, size)
    held_max, held_total, held_position, held_acc = held
    row_max, total, position, acc = scan_keys(left, keys, scores, tile, 0, n_tiles, False, size)
    own_max = held_max[rows, :][:, :1]
    top = jnp.maximum(row_max, own_max)
    here, there = jnp.exp2((own_max - top) * gain), jnp.exp2((row_max - top) * gain)
    finish_tile(
        total * there + held_total[rows, :] * here,
        position * there + held_position[rows, :] * here,
        acc * there + held_acc[rows, :] * here,
        own, disp_ref, tile, n_tiles, size,
    )


def kernel(
    n_rows, size, chunk,
    left_hbm, right_hbm, weight_hbm,
    disp_ref, out_ref,
    left, keys, weight, scores, own, near, far, made, given, edges, sums, parts,
    held_max, held_total, held_position, held_acc,
    load_sem, send_sem, key_sem, raw_x_sem, raw_y_sem, far_sem, given_sem, edge_sem,
):
    length, chans = left.shape
    half = length // 2
    n_tiles, n_chunks = length // size, half // chunk
    bf16 = jnp.bfloat16
    r, w = lax.axis_index("rows"), lax.axis_index("width")
    odd = r % 2
    other_w = 1 - w
    x_row = r + 1 - 2 * odd
    x_tap, far_tap = 2 - 2 * odd, 2 * odd
    below, above = r >= 2, r + 2 < n_rows
    ahead, behind = r - 2 + 4 * odd, r + 2 - 4 * odd
    to_ahead = ((odd == 1) & above) | ((odd == 0) & below)
    to_behind = ((odd == 1) & below) | ((odd == 0) & above)

    load_left = pltpu.make_async_copy(left_hbm.at[0], left, load_sem.at[0])
    load_right = pltpu.make_async_copy(
        right_hbm.at[0], keys.at[pl.ds(w * length, length)], load_sem.at[1]
    )
    load_weight = pltpu.make_async_copy(weight_hbm, weight, load_sem.at[2])
    load_left.start()
    load_right.start()
    load_weight.start()

    barrier = pltpu.get_barrier_semaphore()
    for there in ((r, other_w), (x_row, w)):
        pl.semaphore_signal(barrier, inc=1, device_id=there, device_id_type=MESH)

    @pl.when(below)
    def _():
        pl.semaphore_signal(barrier, inc=1, device_id=(r - 2, w), device_id_type=MESH)

    @pl.when(above)
    def _():
        pl.semaphore_signal(barrier, inc=1, device_id=(r + 2, w), device_id_type=MESH)

    def all_in():
        pl.semaphore_wait(barrier, 2 + below.astype(jnp.int32) + above.astype(jnp.int32))

    def remote(src, dst, sent, received, row, col):
        return pltpu.make_async_remote_copy(
            src_ref=src, dst_ref=dst, send_sem=send_sem.at[sent], recv_sem=received,
            device_id=(row, col), device_id_type=MESH,
        )

    def at16(start, n):
        return pl.ds(pl.multiple_of(start, EDGE), n)

    outer, inner = w * half, (1 - w) * half
    edge_at = (1 - w) * (length - EDGE)

    def part(base, k):
        return at16(base + k * chunk, chunk)

    def raw_x(k):
        here = part(outer, k)
        return remote(own.at[here], near.at[here], 1, raw_x_sem.at[k], x_row, w)

    def raw_y(k):
        here = part(inner, k)
        return remote(own.at[here], near.at[here], 2, raw_y_sem.at[k], ahead, w)

    def hand(k):
        here = part(outer, k)
        return remote(near.at[here], far.at[here], 3, far_sem.at[k], behind, w)

    def sum_copy(here, k):
        return remote(made.at[here], given.at[here], 4, given_sem.at[k], x_row, w)

    def edge_copy(j):
        src = own if j == 0 else near
        return remote(
            src.at[at16(edge_at, EDGE)], edges.at[j], 5, edge_sem.at[j], r, other_w
        )

    def span(base, k):
        if isinstance(k, int) and k == 0:
            return base + EDGE, chunk - 2 * EDGE
        return base + k * chunk - EDGE, chunk

    side_at = half - EDGE
    key_copy = remote(
        right_hbm.at[0], keys.at[pl.ds(0, length)], 0, key_sem.at[0], r, other_w
    )

    def dots(value, tap):
        return [
            jnp.dot(value, weight[tap, b], preferred_element_type=jnp.float32) for b in range(3)
        ]

    def put(ref, base, k, values):
        for b in range(3):
            ref[b, at16(EDGE + base + k * chunk, chunk), :] = values[b]

    def add(ref, base, k, values):
        for b in range(3):
            here = at16(EDGE + base + k * chunk, chunk)
            ref[b, here, :] = ref[b, here, :] + values[b]

    def shifted(ref, start, n):
        before = ref[0, pl.ds(pl.multiple_of(start + EDGE - 8, 8), n + 8), :]
        after = ref[2, at16(start + EDGE, n + 8), :]
        return (
            pltpu.roll(before, 1, 0)[8:, :]
            + ref[1, at16(start + EDGE, n), :]
            + pltpu.roll(after, n + 7, 0)[:n, :]
        )

    def emit(start, n, with_given):
        here = at16(start, n)
        total = shifted(sums, start, n)
        if with_given:
            total = total + given[here, :].astype(jnp.float32)
        out_ref[0, here, :] = total.astype(bf16)

    def give(start, n, k):
        here = at16(start, n)
        made[here, :] = shifted(parts, start, n).astype(bf16)
        sum_copy(here, k).start()

    def loop(body):
        body(0)
        lax.fori_loop(1, n_chunks, lambda k, _: (body(k), 0)[1], 0)

    def prepare(k, _):
        put(sums, outer, k, dots(own[part(outer, k), :], 1))
        value = own[part(inner, k), :]
        put(sums, inner, k, dots(value, 1))
        put(parts, inner, k, dots(value, far_tap))
        return 0

    def take_x(k):
        raw_x(k).wait_recv()

        @pl.when(to_behind)
        def _():
            hand(k).start()

        add(sums, outer, k, dots(near[part(outer, k), :], x_tap))

    def take_y(k):
        @pl.when(to_behind)
        def _():
            raw_y(k).wait_recv()

            @pl.when(k == (1 - w) * (n_chunks - 1))
            def _():
                edge_copy(1).start()

            add(parts, inner, k, dots(near[part(inner, k), :], x_tap))

        give(*span(inner, k), k)

    def take_far(k):
        @pl.when(to_ahead)
        def _():
            hand(k).wait_recv()
            add(sums, outer, k, dots(far[part(outer, k), :], far_tap))

        emit(*span(outer, k), False)

    def take_given(k):
        start, n = span(inner, k)
        sum_copy(at16(start, n), k).wait_recv()
        emit(start, n, True)

    def clear():
        zeros = jnp.zeros((EDGE, chans), jnp.float32)
        sums[0, pl.ds(0, EDGE), :] = zeros
        sums[2, pl.ds(EDGE + length, EDGE), :] = zeros
        for b in range(3):
            for k in range(2):
                parts[b, at16(EDGE + half - (2 - k) * EDGE + 2 * w * EDGE, EDGE), :] = zeros

    def rim():
        edge_copy(0).wait_recv()
        tap_col = 2 - 2 * w
        ours = jnp.dot(edges[0], weight[1, tap_col], preferred_element_type=jnp.float32)
        theirs = jnp.dot(edges[0], weight[far_tap, tap_col], preferred_element_type=jnp.float32)
        here = at16(other_w * (EDGE + length), EDGE)
        sums[tap_col, here, :] = ours
        parts[tap_col, here, :] = theirs

        @pl.when(to_behind)
        def _():
            edge_copy(1).wait_recv()
            parts[tap_col, here, :] = theirs + jnp.dot(
                edges[1], weight[x_tap, tap_col], preferred_element_type=jnp.float32
            )

        give(side_at, 2 * EDGE, n_chunks)
        give(edge_at, EDGE, n_chunks + 1)

    held = (held_max, held_total, held_position, held_acc)
    per_tile = size // chunk

    def send_tile(tile, is_inner):
        for k in range(tile * per_tile, (tile + 1) * per_tile):
            if not is_inner:
                raw_x(k % n_chunks).start()
            else:

                @pl.when(to_ahead)
                def _():
                    raw_y(k % n_chunks).start()

    def mixed(lag):
        take_y(0)

        def step(k, _):
            @pl.when(k < n_chunks)
            def _():
                take_y(k)

            @pl.when(k >= lag)
            def _():
                take_x(k - lag)

            return 0

        lax.fori_loop(1, n_chunks + lag, step, 0)

    @pl.when(w == 0)
    def _():
        all_in()
        key_copy.start()
        load_left.wait()
        load_right.wait()
        for k in range(n_tiles // 2):
            for tile in (k, n_tiles // 2 + k):
                attend_all(left, keys, scores, own, disp_ref, tile, size)
                send_tile(tile, tile >= n_tiles // 2)
        edge_copy(0).start()
        load_weight.wait()
        clear()
        lax.fori_loop(0, n_chunks, prepare, 0)
        mixed(1)

    @pl.when(w == 1)
    def _():
        load_left.wait()
        load_right.wait()
        for tile in range(n_tiles):
            attend_own(left, keys, scores, held, tile, n_tiles, size)
        load_weight.wait()
        clear()
        all_in()
        key_copy.wait_recv()
        for tile in range(n_tiles):
            attend_rest(left, keys, scores, held, own, disp_ref, tile, n_tiles, size)
            if tile == 0:
                edge_copy(0).start()
            send_tile(tile, tile < n_tiles // 2)
        lax.fori_loop(0, n_chunks, prepare, 0)
        mixed(1)

    rim()

    def last(k):
        take_far(k)
        take_given(k)

    loop(last)
    sum_copy(at16(edge_at, EDGE), n_chunks + 1).wait_recv()
    emit(w * (length - EDGE), EDGE, False)
    emit(edge_at, EDGE, True)
    sum_copy(at16(side_at, 2 * EDGE), n_chunks).wait_recv()
    emit(side_at, 2 * EDGE, True)

    def sent(ref, n, which):
        remote(ref.at[pl.ds(0, n)], ref.at[pl.ds(0, n)], which, key_sem.at[0], x_row, w).wait_send()

    @pl.when(w == 0)
    def _():
        key_copy.wait_send()

    sent(own, half, 1)
    sent(made, half + EDGE, 4)
    sent(edges, 1, 5)

    @pl.when(to_ahead)
    def _():
        sent(own, half, 2)

    @pl.when(to_behind)
    def _():
        sent(near, half, 3)
        sent(edges, 1, 5)


def hand_on(disp_in, out_in, disp_ref, out_ref, sem):
    copies = [
        pltpu.make_async_copy(out_in, out_ref, sem.at[0]),
        pltpu.make_async_copy(disp_in, disp_ref, sem.at[1]),
    ]
    for copy in copies:
        copy.start()
    for copy in copies:
        copy.wait()


def fused(n_rows, left_feat, right_feat, refine_weight):
    _, length, chans = left_feat.shape
    half = length // 2
    size = math.gcd(half, 256)
    chunk = math.gcd(size, CHUNK)
    n_chunks = half // chunk
    bf16, f32 = jnp.bfloat16, jnp.float32
    dma = pltpu.SemaphoreType.DMA
    rows = pltpu.VMEM((length, chans), bf16)
    found = pl.pallas_call(
        functools.partial(kernel, n_rows, size, chunk),
        out_shape=(pltpu.VMEM((1, length), f32), pltpu.VMEM((1, length, chans), bf16)),
        in_specs=[pl.BlockSpec(memory_space=pltpu.HBM)] * 3,
        out_specs=[pl.BlockSpec(memory_space=pltpu.VMEM)] * 2,
        scratch_shapes=[
            rows,
            pltpu.VMEM((2 * length, chans), bf16),
            pltpu.VMEM((3, 3, chans, chans), bf16),
            pltpu.VMEM((size, 2 * length), f32),
            rows,
            rows,
            rows,
            rows,
            rows,
            pltpu.VMEM((2, EDGE, chans), bf16),
            pltpu.VMEM((3, length + 2 * EDGE, chans), f32),
            pltpu.VMEM((3, length + 2 * EDGE, chans), f32),
            pltpu.VMEM((length, LANES), f32),
            pltpu.VMEM((length, LANES), f32),
            pltpu.VMEM((length, LANES), f32),
            pltpu.VMEM((length, chans), f32),
            dma((3,)),
            dma((6,)),
            dma((1,)),
            dma((n_chunks,)),
            dma((n_chunks,)),
            dma((n_chunks,)),
            dma((n_chunks + 2,)),
            dma((2,)),
        ],
        compiler_params=pltpu.CompilerParams(
            collective_id=0, has_side_effects=True, vmem_limit_bytes=VMEM_LIMIT
        ),
    )(*(pltpu.with_memory_space_constraint(x, pltpu.HBM) for x in (left_feat, right_feat, refine_weight)))
    return pl.pallas_call(
        hand_on,
        out_shape=(
            jax.ShapeDtypeStruct((1, length), f32),
            jax.ShapeDtypeStruct((1, length, chans), bf16),
        ),
        in_specs=[pl.BlockSpec(memory_space=pltpu.VMEM)] * 2,
        out_specs=[pl.BlockSpec(memory_space=pltpu.HBM)] * 2,
        scratch_shapes=[dma((2,))],
        compiler_params=pltpu.CompilerParams(vmem_limit_bytes=VMEM_LIMIT),
    )(*found)


def solution(mesh):
    n_rows, n_width = mesh.shape["rows"], mesh.shape["width"]

    def local(left_feat, right_feat, refine_weight):
        rows_here, length, chans = left_feat.shape
        fits = n_rows % 2 == 0 and n_width == 2 and rows_here == 1
        if fits and length % (2 * CHUNK) == 0 and chans % LANES == 0:
            return fused(n_rows, left_feat, right_feat, refine_weight)
        return body(left_feat, right_feat, refine_weight)

    placed = (P("rows", "width", None), P("rows", "width", None), P())
    return jax.shard_map(
        local,
        mesh=mesh,
        in_specs=placed,
        out_specs=(P("rows", "width"), P("rows", "width", None)),
        check_vma=False,
    )
```

```python
import functools
import math

import jax
import jax.numpy as jnp
from jax import lax
from jax.experimental import pallas as pl
from jax.experimental.pallas import tpu as pltpu
from jax.sharding import PartitionSpec as P

NEG_FILL = -1e30


def extended(value, sides, width):
    for axis, dim in sides:
        size, length = (lax.axis_size(axis), value.shape[dim])
        up = [(i, (i + 1) % size) for i in range(size - 1)]
        down = [(j, i) for i, j in up]
        last = lax.slice_in_dim(value, length - width, length, axis=dim)
        leading = lax.slice_in_dim(value, 0, width, axis=dim)
        before = lax.ppermute(last, axis, up)
        after = lax.ppermute(leading, axis, down)
        value = jnp.concatenate([before, value, after], axis=dim)
    return value


def absorb_block(state_now, query_rows, query_positions, sub_keys, key_positions):
    run_max, run_total, weighted, position_sum = state_now
    score_scale = 1.0 / math.sqrt(query_rows.shape[-1])
    scores = (
        jnp.einsum("rqc,rkc->rqk", query_rows, sub_keys, preferred_element_type=jnp.float32)
        * score_scale
    )
    allowed = (key_positions[None, :] <= query_positions[:, None]) & (key_positions[None, :] >= 0)
    scores = jnp.where(allowed[None], scores, NEG_FILL)
    new_max = jnp.maximum(run_max, scores.max(-1))
    factor = jnp.exp(run_max - new_max)
    weights = jnp.where(allowed[None], jnp.exp(scores - new_max[..., None]), 0.0)
    run_total = run_total * factor + weights.sum(-1)
    weighted = weighted * factor[..., None] + jnp.einsum(
        "rqk,rkc->rqc", weights.astype(jnp.bfloat16), sub_keys, preferred_element_type=jnp.float32
    )
    position_sum = position_sum * factor + (
        weights * key_positions.astype(jnp.float32)[None, None, :]
    ).sum(-1)
    return (new_max, run_total, weighted, position_sum)


def absorb_piece(state_now, query_rows, query_positions, key_piece):
    n_keys = key_piece.shape[1]
    sub_len = math.gcd(n_keys, 512)
    count = n_keys // sub_len
    last_query = query_positions[-1]

    def one_sub(carry_state, sub_index):
        sub_start = sub_index * sub_len
        sub_keys = lax.dynamic_slice_in_dim(key_piece, sub_index * sub_len, sub_len, 1)
        key_positions = sub_start + jnp.arange(sub_len, dtype=jnp.int32)
        result_state = lax.cond(
            sub_start <= last_query,
            lambda inner: absorb_block(inner, query_rows, query_positions, sub_keys, key_positions),
            lambda inner: inner,
            carry_state,
        )
        return (result_state, None)

    result, _ = lax.scan(one_sub, state_now, jnp.arange(count, dtype=jnp.int32))
    return result


def empty_state(rows_here, length, chans):
    return (
        jnp.full((rows_here, length), NEG_FILL, jnp.float32),
        jnp.zeros((rows_here, length), jnp.float32),
        jnp.zeros((rows_here, length, chans), jnp.float32),
        jnp.zeros((rows_here, length), jnp.float32),
    )


def finish_state(state_now, query_positions):
    run_max, run_total, weighted, position_sum = state_now
    matched = (weighted / run_total[..., None]).astype(jnp.bfloat16)
    disparity = query_positions.astype(jnp.float32)[None, :] - position_sum / run_total
    return (matched, disparity)


def body(left_feat, right_feat, refine_weight):
    rows_here, block_len, chans = left_feat.shape
    my_index = lax.axis_index("width")
    offset = my_index * block_len
    query_positions = offset + jnp.arange(block_len, dtype=jnp.int32)
    final_state = absorb_piece(
        empty_state(rows_here, block_len, chans),
        left_feat,
        query_positions,
        lax.all_gather(right_feat, "width", axis=1, tiled=True),
    )
    matched, disparity = finish_state(final_state, query_positions)
    padded = extended(matched, (("rows", 0), ("width", 1)), 1)
    total = jnp.zeros((rows_here * block_len, chans), jnp.float32)
    for tap_row in range(3):
        for tap_col in range(3):
            window = padded[tap_row : tap_row + rows_here, tap_col : tap_col + block_len].reshape(
                -1, chans
            )
            total = total + jnp.dot(
                window, refine_weight[tap_row, tap_col], preferred_element_type=jnp.float32
            )
    refined = total.reshape(rows_here, block_len, chans).astype(jnp.bfloat16)
    return (disparity, refined)


MESH = pl.DeviceIdType.MESH
EDGE = 16
LANES = 128
CHUNK = 128
VMEM_LIMIT = 32 * 1024 * 1024


def scan_keys(left, keys, scores, tile, first, n_tiles, masked, size):
    chans = left.shape[-1]
    gain = math.log2(math.e) / math.sqrt(chans)
    queries = left[pl.ds(tile * size, size), :]
    lane_max = jnp.full((size, LANES), NEG_FILL, jnp.float32)
    for kt in range(n_tiles):
        s = lax.dot_general(
            queries,
            keys[pl.ds((first + kt) * size, size), :],
            (((1,), (1,)), ((), ())),
            preferred_element_type=jnp.float32,
        )
        if masked and kt == n_tiles - 1:
            q_at = lax.broadcasted_iota(jnp.int32, (size, size), 0)
            k_at = lax.broadcasted_iota(jnp.int32, (size, size), 1)
            s = jnp.where(k_at <= q_at, s, NEG_FILL)
        scores[:, pl.ds(kt * size, size)] = s
        for c in range(0, size, LANES):
            lane_max = jnp.maximum(lane_max, s[:, c : c + LANES])
    row_max = jnp.max(lane_max, axis=1, keepdims=True)
    total = jnp.zeros((size, LANES), jnp.float32)
    prefix = jnp.zeros((size, LANES), jnp.float32)
    acc = jnp.zeros((size, chans), jnp.float32)
    for kt in range(n_tiles):
        p = jnp.exp2((scores[:, pl.ds(kt * size, size)] - row_max) * gain)
        for c in range(0, size, LANES):
            total = total + p[:, c : c + LANES]
            prefix = prefix + total
        acc = acc + jnp.dot(
            p.astype(jnp.bfloat16),
            keys[pl.ds((first + kt) * size, size), :],
            preferred_element_type=jnp.float32,
        )
    n_chunks = n_tiles * (size // LANES)
    lane = lax.broadcasted_iota(jnp.int32, (size, LANES), 1).astype(jnp.float32)
    position = LANES * (n_chunks * total - prefix) + (lane + first * size) * total
    return row_max, total, position, acc


def finish_tile(total, position, acc, own, disp_ref, tile, first_query_tile, size):
    rows = pl.ds(tile * size, size)
    denominator = jnp.sum(total, axis=1, keepdims=True)
    own[rows, :] = (acc * (1.0 / denominator)).astype(jnp.bfloat16)
    total_t = jnp.sum(total.T, axis=0, keepdims=True)
    position_t = jnp.sum(position.T, axis=0, keepdims=True)
    at = lax.broadcasted_iota(jnp.int32, (1, size), 1) + (first_query_tile + tile) * size
    disp_ref[:, rows] = at.astype(jnp.float32) - position_t / total_t


def attend_all(left, keys, scores, own, disp_ref, tile, size):
    _, *found = scan_keys(left, keys, scores, tile, 0, tile + 1, True, size)
    finish_tile(*found, own, disp_ref, tile, 0, size)


def attend_own(left, keys, scores, held, tile, n_tiles, size):
    rows = pl.ds(tile * size, size)
    held_max, held_total, held_position, held_acc = held
    row_max, total, position, acc = scan_keys(
        left, keys, scores, tile, n_tiles, tile + 1, True, size
    )
    held_max[rows, :] = jnp.broadcast_to(row_max, total.shape)
    held_total[rows, :] = total
    held_position[rows, :] = position
    held_acc[rows, :] = acc


def attend_rest(left, keys, scores, held, own, disp_ref, tile, n_tiles, size):
    gain = math.log2(math.e) / math.sqrt(left.shape[-1])
    rows = pl.ds(tile * size, size)
    held_max, held_total, held_position, held_acc = held
    row_max, total, position, acc = scan_keys(left, keys, scores, tile, 0, n_tiles, False, size)
    own_max = held_max[rows, :][:, :1]
    top = jnp.maximum(row_max, own_max)
    here, there = jnp.exp2((own_max - top) * gain), jnp.exp2((row_max - top) * gain)
    finish_tile(
        total * there + held_total[rows, :] * here,
        position * there + held_position[rows, :] * here,
        acc * there + held_acc[rows, :] * here,
        own, disp_ref, tile, n_tiles, size,
    )


def kernel(
    n_rows, size, chunk,
    left_hbm, right_hbm, weight_hbm,
    disp_ref, out_ref,
    left, keys, weight, scores, own, near, far, made, given, edges, sums, parts,
    held_max, held_total, held_position, held_acc,
    load_sem, send_sem, key_sem, raw_x_sem, raw_y_sem, far_sem, given_sem, edge_sem,
):
    length, chans = left.shape
    half = length // 2
    n_tiles, n_chunks = length // size, half // chunk
    bf16 = jnp.bfloat16
    r, w = lax.axis_index("rows"), lax.axis_index("width")
    odd = r % 2
    other_w = 1 - w
    x_row = r + 1 - 2 * odd
    x_tap, far_tap = 2 - 2 * odd, 2 * odd
    below, above = r >= 2, r + 2 < n_rows
    ahead, behind = r - 2 + 4 * odd, r + 2 - 4 * odd
    to_ahead = ((odd == 1) & above) | ((odd == 0) & below)
    to_behind = ((odd == 1) & below) | ((odd == 0) & above)

    def load_left(k):
        here = pl.ds(k * size, size)
        return pltpu.make_async_copy(left_hbm.at[0, here], left.at[here], load_sem.at[0, k])

    def load_right(k):
        there = pl.ds(pl.multiple_of(w * length + k * size, size), size)
        return pltpu.make_async_copy(
            right_hbm.at[0, pl.ds(k * size, size)], keys.at[there], load_sem.at[1, k]
        )

    load_weight = pltpu.make_async_copy(weight_hbm, weight, load_sem.at[2, 0])
    for k in range(n_tiles):
        load_left(k).start()
        load_right(k).start()

    barrier = pltpu.get_barrier_semaphore()
    for there in ((r, other_w), (x_row, w)):
        pl.semaphore_signal(barrier, inc=1, device_id=there, device_id_type=MESH)

    @pl.when(below)
    def _():
        pl.semaphore_signal(barrier, inc=1, device_id=(r - 2, w), device_id_type=MESH)

    @pl.when(above)
    def _():
        pl.semaphore_signal(barrier, inc=1, device_id=(r + 2, w), device_id_type=MESH)

    def all_in():
        pl.semaphore_wait(barrier, 2 + below.astype(jnp.int32) + above.astype(jnp.int32))

    def remote(src, dst, sent, received, row, col):
        return pltpu.make_async_remote_copy(
            src_ref=src, dst_ref=dst, send_sem=send_sem.at[sent], recv_sem=received,
            device_id=(row, col), device_id_type=MESH,
        )

    def at16(start, n):
        return pl.ds(pl.multiple_of(start, EDGE), n)

    outer, inner = w * half, (1 - w) * half
    edge_at = (1 - w) * (length - EDGE)

    def part(base, k):
        return at16(base + k * chunk, chunk)

    def raw_x(k):
        here = part(outer, k)
        return remote(own.at[here], near.at[here], 1, raw_x_sem.at[k], x_row, w)

    def raw_y(k):
        here = part(inner, k)
        return remote(own.at[here], near.at[here], 2, raw_y_sem.at[k], ahead, w)

    def hand(k):
        here = part(outer, k)
        return remote(near.at[here], far.at[here], 3, far_sem.at[k], behind, w)

    def sum_copy(here, k):
        return remote(made.at[here], given.at[here], 4, given_sem.at[k], x_row, w)

    def edge_copy(j):
        src = own if j == 0 else near
        return remote(
            src.at[at16(edge_at, EDGE)], edges.at[j], 5, edge_sem.at[j], r, other_w
        )

    def span(base, k):
        if isinstance(k, int) and k == 0:
            return base + EDGE, chunk - 2 * EDGE
        return base + k * chunk - EDGE, chunk

    side_at = half - EDGE
    key_copy = remote(
        right_hbm.at[0], keys.at[pl.ds(0, length)], 0, key_sem.at[0], r, other_w
    )

    def dots(value, tap):
        return [
            jnp.dot(value, weight[tap, b], preferred_element_type=jnp.float32) for b in range(3)
        ]

    def put(ref, base, k, values):
        for b in range(3):
            ref[b, at16(EDGE + base + k * chunk, chunk), :] = values[b]

    def add(ref, base, k, values):
        for b in range(3):
            here = at16(EDGE + base + k * chunk, chunk)
            ref[b, here, :] = ref[b, here, :] + values[b]

    def shifted(ref, start, n):
        before = ref[0, pl.ds(pl.multiple_of(start + EDGE - 8, 8), n + 8), :]
        after = ref[2, at16(start + EDGE, n + 8), :]
        return (
            pltpu.roll(before, 1, 0)[8:, :]
            + ref[1, at16(start + EDGE, n), :]
            + pltpu.roll(after, n + 7, 0)[:n, :]
        )

    def emit(start, n, with_given):
        here = at16(start, n)
        total = shifted(sums, start, n)
        if with_given:
            total = total + given[here, :].astype(jnp.float32)
        out_ref[0, here, :] = total.astype(bf16)

    def give(start, n, k):
        here = at16(start, n)
        made[here, :] = shifted(parts, start, n).astype(bf16)
        sum_copy(here, k).start()

    def loop(body):
        body(0)
        lax.fori_loop(1, n_chunks, lambda k, _: (body(k), 0)[1], 0)

    def prepare(k, _):
        put(sums, outer, k, dots(own[part(outer, k), :], 1))
        value = own[part(inner, k), :]
        put(sums, inner, k, dots(value, 1))
        put(parts, inner, k, dots(value, far_tap))
        return 0

    def take_x(k):
        raw_x(k).wait_recv()

        @pl.when(to_behind)
        def _():
            hand(k).start()

        add(sums, outer, k, dots(near[part(outer, k), :], x_tap))

    def take_y(k):
        @pl.when(to_behind)
        def _():
            raw_y(k).wait_recv()

            @pl.when(k == (1 - w) * (n_chunks - 1))
            def _():
                edge_copy(1).start()

            add(parts, inner, k, dots(near[part(inner, k), :], x_tap))

        give(*span(inner, k), k)

    def take_far(k):
        @pl.when(to_ahead)
        def _():
            hand(k).wait_recv()
            add(sums, outer, k, dots(far[part(outer, k), :], far_tap))

        emit(*span(outer, k), False)

    def take_given(k):
        start, n = span(inner, k)
        sum_copy(at16(start, n), k).wait_recv()
        emit(start, n, True)

    def clear():
        zeros = jnp.zeros((EDGE, chans), jnp.float32)
        sums[0, pl.ds(0, EDGE), :] = zeros
        sums[2, pl.ds(EDGE + length, EDGE), :] = zeros
        for b in range(3):
            for k in range(2):
                parts[b, at16(EDGE + half - (2 - k) * EDGE + 2 * w * EDGE, EDGE), :] = zeros

    def rim():
        edge_copy(0).wait_recv()
        tap_col = 2 - 2 * w
        ours = jnp.dot(edges[0], weight[1, tap_col], preferred_element_type=jnp.float32)
        theirs = jnp.dot(edges[0], weight[far_tap, tap_col], preferred_element_type=jnp.float32)
        here = at16(other_w * (EDGE + length), EDGE)
        sums[tap_col, here, :] = ours
        parts[tap_col, here, :] = theirs

        @pl.when(to_behind)
        def _():
            edge_copy(1).wait_recv()
            parts[tap_col, here, :] = theirs + jnp.dot(
                edges[1], weight[x_tap, tap_col], preferred_element_type=jnp.float32
            )

        give(side_at, 2 * EDGE, n_chunks)
        give(edge_at, EDGE, n_chunks + 1)

    held = (held_max, held_total, held_position, held_acc)
    per_tile = size // chunk

    def send_tile(tile, is_inner):
        for k in range(tile * per_tile, (tile + 1) * per_tile):
            if not is_inner:
                raw_x(k % n_chunks).start()
            else:

                @pl.when(to_ahead)
                def _():
                    raw_y(k % n_chunks).start()

    def mixed(lag):
        take_y(0)

        def step(k, _):
            @pl.when(k < n_chunks)
            def _():
                take_y(k)

            @pl.when(k >= lag)
            def _():
                take_x(k - lag)

            return 0

        lax.fori_loop(1, n_chunks + lag, step, 0)

    @pl.when(w == 0)
    def _():
        load_weight.start()
        loaded = 0
        for at in range(n_tiles):
            tile = at // 2 + at % 2 * (n_tiles // 2)
            for k in range(loaded, tile + 1):
                load_left(k).wait()
                load_right(k).wait()
            loaded = max(loaded, tile + 1)
            attend_all(left, keys, scores, own, disp_ref, tile, size)
            if at == 0:
                all_in()
                key_copy.start()
            send_tile(tile, tile >= n_tiles // 2)
        edge_copy(0).start()
        load_weight.wait()
        clear()
        lax.fori_loop(0, n_chunks, prepare, 0)
        mixed(1)

    @pl.when(w == 1)
    def _():
        load_weight.start()
        for tile in range(n_tiles):
            load_left(tile).wait()
            load_right(tile).wait()
            attend_own(left, keys, scores, held, tile, n_tiles, size)
        load_weight.wait()
        clear()
        all_in()
        key_copy.wait_recv()
        for tile in range(n_tiles):
            attend_rest(left, keys, scores, held, own, disp_ref, tile, n_tiles, size)
            if tile == 0:
                edge_copy(0).start()
            send_tile(tile, tile < n_tiles // 2)
        lax.fori_loop(0, n_chunks, prepare, 0)
        mixed(1)

    rim()

    def last(k):
        take_far(k)
        take_given(k)

    loop(last)
    sum_copy(at16(edge_at, EDGE), n_chunks + 1).wait_recv()
    emit(w * (length - EDGE), EDGE, False)
    emit(edge_at, EDGE, True)
    sum_copy(at16(side_at, 2 * EDGE), n_chunks).wait_recv()
    emit(side_at, 2 * EDGE, True)

    def sent(ref, n, which):
        remote(ref.at[pl.ds(0, n)], ref.at[pl.ds(0, n)], which, key_sem.at[0], x_row, w).wait_send()

    @pl.when(w == 0)
    def _():
        key_copy.wait_send()

    sent(own, half, 1)
    sent(made, half + EDGE, 4)
    sent(edges, 1, 5)

    @pl.when(to_ahead)
    def _():
        sent(own, half, 2)

    @pl.when(to_behind)
    def _():
        sent(near, half, 3)
        sent(edges, 1, 5)


def hand_on(disp_in, out_in, disp_ref, out_ref, sem):
    copies = [
        pltpu.make_async_copy(out_in, out_ref, sem.at[0]),
        pltpu.make_async_copy(disp_in, disp_ref, sem.at[1]),
    ]
    for copy in copies:
        copy.start()
    for copy in copies:
        copy.wait()


def fused(n_rows, left_feat, right_feat, refine_weight):
    _, length, chans = left_feat.shape
    half = length // 2
    size = math.gcd(half, 256)
    chunk = math.gcd(size, CHUNK)
    n_chunks = half // chunk
    bf16, f32 = jnp.bfloat16, jnp.float32
    dma = pltpu.SemaphoreType.DMA
    rows = pltpu.VMEM((length, chans), bf16)
    found = pl.pallas_call(
        functools.partial(kernel, n_rows, size, chunk),
        out_shape=(pltpu.VMEM((1, length), f32), pltpu.VMEM((1, length, chans), bf16)),
        in_specs=[pl.BlockSpec(memory_space=pltpu.HBM)] * 3,
        out_specs=[pl.BlockSpec(memory_space=pltpu.VMEM)] * 2,
        scratch_shapes=[
            rows,
            pltpu.VMEM((2 * length, chans), bf16),
            pltpu.VMEM((3, 3, chans, chans), bf16),
            pltpu.VMEM((size, 2 * length), f32),
            rows,
            rows,
            rows,
            rows,
            rows,
            pltpu.VMEM((2, EDGE, chans), bf16),
            pltpu.VMEM((3, length + 2 * EDGE, chans), f32),
            pltpu.VMEM((3, length + 2 * EDGE, chans), f32),
            pltpu.VMEM((length, LANES), f32),
            pltpu.VMEM((length, LANES), f32),
            pltpu.VMEM((length, LANES), f32),
            pltpu.VMEM((length, chans), f32),
            dma((3, length // size)),
            dma((6,)),
            dma((1,)),
            dma((n_chunks,)),
            dma((n_chunks,)),
            dma((n_chunks,)),
            dma((n_chunks + 2,)),
            dma((2,)),
        ],
        compiler_params=pltpu.CompilerParams(
            collective_id=0, has_side_effects=True, vmem_limit_bytes=VMEM_LIMIT
        ),
    )(*(pltpu.with_memory_space_constraint(x, pltpu.HBM) for x in (left_feat, right_feat, refine_weight)))
    return pl.pallas_call(
        hand_on,
        out_shape=(
            jax.ShapeDtypeStruct((1, length), f32),
            jax.ShapeDtypeStruct((1, length, chans), bf16),
        ),
        in_specs=[pl.BlockSpec(memory_space=pltpu.VMEM)] * 2,
        out_specs=[pl.BlockSpec(memory_space=pltpu.HBM)] * 2,
        scratch_shapes=[dma((2,))],
        compiler_params=pltpu.CompilerParams(vmem_limit_bytes=VMEM_LIMIT),
    )(*found)


def solution(mesh):
    n_rows, n_width = mesh.shape["rows"], mesh.shape["width"]

    def local(left_feat, right_feat, refine_weight):
        rows_here, length, chans = left_feat.shape
        fits = n_rows % 2 == 0 and n_width == 2 and rows_here == 1
        if fits and length % (2 * CHUNK) == 0 and chans % LANES == 0:
            return fused(n_rows, left_feat, right_feat, refine_weight)
        return body(left_feat, right_feat, refine_weight)

    placed = (P("rows", "width", None), P("rows", "width", None), P())
    return jax.shard_map(
        local,
        mesh=mesh,
        in_specs=placed,
        out_specs=(P("rows", "width"), P("rows", "width", None)),
        check_vma=False,
    )
```

```python
import functools
import math

import jax
import jax.numpy as jnp
from jax import lax
from jax.experimental import pallas as pl
from jax.experimental.pallas import tpu as pltpu
from jax.sharding import PartitionSpec as P

NEG_FILL = -1e30


def extended(value, sides, width):
    for axis, dim in sides:
        size, length = (lax.axis_size(axis), value.shape[dim])
        up = [(i, (i + 1) % size) for i in range(size - 1)]
        down = [(j, i) for i, j in up]
        last = lax.slice_in_dim(value, length - width, length, axis=dim)
        leading = lax.slice_in_dim(value, 0, width, axis=dim)
        before = lax.ppermute(last, axis, up)
        after = lax.ppermute(leading, axis, down)
        value = jnp.concatenate([before, value, after], axis=dim)
    return value


def absorb_block(state_now, query_rows, query_positions, sub_keys, key_positions):
    run_max, run_total, weighted, position_sum = state_now
    score_scale = 1.0 / math.sqrt(query_rows.shape[-1])
    scores = (
        jnp.einsum("rqc,rkc->rqk", query_rows, sub_keys, preferred_element_type=jnp.float32)
        * score_scale
    )
    allowed = (key_positions[None, :] <= query_positions[:, None]) & (key_positions[None, :] >= 0)
    scores = jnp.where(allowed[None], scores, NEG_FILL)
    new_max = jnp.maximum(run_max, scores.max(-1))
    factor = jnp.exp(run_max - new_max)
    weights = jnp.where(allowed[None], jnp.exp(scores - new_max[..., None]), 0.0)
    run_total = run_total * factor + weights.sum(-1)
    weighted = weighted * factor[..., None] + jnp.einsum(
        "rqk,rkc->rqc", weights.astype(jnp.bfloat16), sub_keys, preferred_element_type=jnp.float32
    )
    position_sum = position_sum * factor + (
        weights * key_positions.astype(jnp.float32)[None, None, :]
    ).sum(-1)
    return (new_max, run_total, weighted, position_sum)


def absorb_piece(state_now, query_rows, query_positions, key_piece):
    n_keys = key_piece.shape[1]
    sub_len = math.gcd(n_keys, 512)
    count = n_keys // sub_len
    last_query = query_positions[-1]

    def one_sub(carry_state, sub_index):
        sub_start = sub_index * sub_len
        sub_keys = lax.dynamic_slice_in_dim(key_piece, sub_index * sub_len, sub_len, 1)
        key_positions = sub_start + jnp.arange(sub_len, dtype=jnp.int32)
        result_state = lax.cond(
            sub_start <= last_query,
            lambda inner: absorb_block(inner, query_rows, query_positions, sub_keys, key_positions),
            lambda inner: inner,
            carry_state,
        )
        return (result_state, None)

    result, _ = lax.scan(one_sub, state_now, jnp.arange(count, dtype=jnp.int32))
    return result


def empty_state(rows_here, length, chans):
    return (
        jnp.full((rows_here, length), NEG_FILL, jnp.float32),
        jnp.zeros((rows_here, length), jnp.float32),
        jnp.zeros((rows_here, length, chans), jnp.float32),
        jnp.zeros((rows_here, length), jnp.float32),
    )


def finish_state(state_now, query_positions):
    run_max, run_total, weighted, position_sum = state_now
    matched = (weighted / run_total[..., None]).astype(jnp.bfloat16)
    disparity = query_positions.astype(jnp.float32)[None, :] - position_sum / run_total
    return (matched, disparity)


def body(left_feat, right_feat, refine_weight):
    rows_here, block_len, chans = left_feat.shape
    my_index = lax.axis_index("width")
    offset = my_index * block_len
    query_positions = offset + jnp.arange(block_len, dtype=jnp.int32)
    final_state = absorb_piece(
        empty_state(rows_here, block_len, chans),
        left_feat,
        query_positions,
        lax.all_gather(right_feat, "width", axis=1, tiled=True),
    )
    matched, disparity = finish_state(final_state, query_positions)
    padded = extended(matched, (("rows", 0), ("width", 1)), 1)
    total = jnp.zeros((rows_here * block_len, chans), jnp.float32)
    for tap_row in range(3):
        for tap_col in range(3):
            window = padded[tap_row : tap_row + rows_here, tap_col : tap_col + block_len].reshape(
                -1, chans
            )
            total = total + jnp.dot(
                window, refine_weight[tap_row, tap_col], preferred_element_type=jnp.float32
            )
    refined = total.reshape(rows_here, block_len, chans).astype(jnp.bfloat16)
    return (disparity, refined)


MESH = pl.DeviceIdType.MESH
EDGE = 16
LANES = 128
CHUNK = 128
VMEM_LIMIT = 32 * 1024 * 1024


def scan_keys(left, keys, scores, tile, first, n_tiles, masked, size):
    chans = left.shape[-1]
    gain = math.log2(math.e) / math.sqrt(chans)
    queries = left[pl.ds(tile * size, size), :]
    lane_max = jnp.full((size, LANES), NEG_FILL, jnp.float32)
    for kt in range(n_tiles):
        s = lax.dot_general(
            queries,
            keys[pl.ds((first + kt) * size, size), :],
            (((1,), (1,)), ((), ())),
            preferred_element_type=jnp.float32,
        )
        if masked and kt == n_tiles - 1:
            q_at = lax.broadcasted_iota(jnp.int32, (size, size), 0)
            k_at = lax.broadcasted_iota(jnp.int32, (size, size), 1)
            s = jnp.where(k_at <= q_at, s, NEG_FILL)
        scores[:, pl.ds(kt * size, size)] = s
        for c in range(0, size, LANES):
            lane_max = jnp.maximum(lane_max, s[:, c : c + LANES])
    row_max = jnp.max(lane_max, axis=1, keepdims=True)
    total = jnp.zeros((size, LANES), jnp.float32)
    prefix = jnp.zeros((size, LANES), jnp.float32)
    acc = jnp.zeros((size, chans), jnp.float32)
    for kt in range(n_tiles):
        p = jnp.exp2((scores[:, pl.ds(kt * size, size)] - row_max) * gain)
        for c in range(0, size, LANES):
            total = total + p[:, c : c + LANES]
            prefix = prefix + total
        acc = acc + jnp.dot(
            p.astype(jnp.bfloat16),
            keys[pl.ds((first + kt) * size, size), :],
            preferred_element_type=jnp.float32,
        )
    n_chunks = n_tiles * (size // LANES)
    lane = lax.broadcasted_iota(jnp.int32, (size, LANES), 1).astype(jnp.float32)
    position = LANES * (n_chunks * total - prefix) + (lane + first * size) * total
    return row_max, total, position, acc


def finish_tile(total, position, acc, own, disp_ref, tile, first_query_tile, size):
    rows = pl.ds(tile * size, size)
    denominator = jnp.sum(total, axis=1, keepdims=True)
    own[rows, :] = (acc * (1.0 / denominator)).astype(jnp.bfloat16)
    total_t = jnp.sum(total.T, axis=0, keepdims=True)
    position_t = jnp.sum(position.T, axis=0, keepdims=True)
    at = lax.broadcasted_iota(jnp.int32, (1, size), 1) + (first_query_tile + tile) * size
    disp_ref[:, rows] = at.astype(jnp.float32) - position_t / total_t


def attend_all(left, keys, scores, own, disp_ref, tile, size):
    _, *found = scan_keys(left, keys, scores, tile, 0, tile + 1, True, size)
    finish_tile(*found, own, disp_ref, tile, 0, size)


def attend_own(left, keys, scores, held, tile, n_tiles, size):
    rows = pl.ds(tile * size, size)
    held_max, held_total, held_position, held_acc = held
    row_max, total, position, acc = scan_keys(
        left, keys, scores, tile, n_tiles, tile + 1, True, size
    )
    held_max[rows, :] = jnp.broadcast_to(row_max, total.shape)
    held_total[rows, :] = total
    held_position[rows, :] = position
    held_acc[rows, :] = acc


def attend_rest(left, keys, scores, held, own, disp_ref, tile, n_tiles, size):
    gain = math.log2(math.e) / math.sqrt(left.shape[-1])
    rows = pl.ds(tile * size, size)
    held_max, held_total, held_position, held_acc = held
    row_max, total, position, acc = scan_keys(left, keys, scores, tile, 0, n_tiles, False, size)
    own_max = held_max[rows, :][:, :1]
    top = jnp.maximum(row_max, own_max)
    here, there = jnp.exp2((own_max - top) * gain), jnp.exp2((row_max - top) * gain)
    finish_tile(
        total * there + held_total[rows, :] * here,
        position * there + held_position[rows, :] * here,
        acc * there + held_acc[rows, :] * here,
        own, disp_ref, tile, n_tiles, size,
    )


def kernel(
    n_rows, size, chunk,
    left_hbm, right_hbm, weight_hbm,
    disp_ref, out_ref,
    left, keys, weight, scores, own, near, far, made, given, edges, sums, parts,
    held_max, held_total, held_position, held_acc,
    load_sem, send_sem, key_sem, raw_x_sem, raw_y_sem, far_sem, given_sem, edge_sem,
):
    length, chans = left.shape
    half = length // 2
    n_tiles, n_chunks = length // size, half // chunk
    bf16 = jnp.bfloat16
    r, w = lax.axis_index("rows"), lax.axis_index("width")
    odd = r % 2
    other_w = 1 - w
    x_row = r + 1 - 2 * odd
    x_tap, far_tap = 2 - 2 * odd, 2 * odd
    below, above = r >= 2, r + 2 < n_rows
    ahead, behind = r - 2 + 4 * odd, r + 2 - 4 * odd
    to_ahead = ((odd == 1) & above) | ((odd == 0) & below)
    to_behind = ((odd == 1) & below) | ((odd == 0) & above)

    pieces = ((0, size), (size, length - size))

    def load_left(k):
        here = pl.ds(*pieces[k])
        return pltpu.make_async_copy(left_hbm.at[0, here], left.at[here], load_sem.at[k])

    def load_right(k):
        start, n = pieces[k]
        there = pl.ds(pl.multiple_of(w * length + start, size), n)
        return pltpu.make_async_copy(
            right_hbm.at[0, pl.ds(start, n)], keys.at[there], load_sem.at[2 + k]
        )

    load_weight = pltpu.make_async_copy(weight_hbm, weight, load_sem.at[4])
    for k in range(2):
        load_left(k).start()
        load_right(k).start()

    def loaded(k):
        load_left(k).wait()
        load_right(k).wait()

    barrier = pltpu.get_barrier_semaphore()
    for there in ((r, other_w), (x_row, w)):
        pl.semaphore_signal(barrier, inc=1, device_id=there, device_id_type=MESH)

    @pl.when(below)
    def _():
        pl.semaphore_signal(barrier, inc=1, device_id=(r - 2, w), device_id_type=MESH)

    @pl.when(above)
    def _():
        pl.semaphore_signal(barrier, inc=1, device_id=(r + 2, w), device_id_type=MESH)

    def all_in():
        pl.semaphore_wait(barrier, 2 + below.astype(jnp.int32) + above.astype(jnp.int32))

    def remote(src, dst, sent, received, row, col):
        return pltpu.make_async_remote_copy(
            src_ref=src, dst_ref=dst, send_sem=send_sem.at[sent], recv_sem=received,
            device_id=(row, col), device_id_type=MESH,
        )

    def at16(start, n):
        return pl.ds(pl.multiple_of(start, EDGE), n)

    outer, inner = w * half, (1 - w) * half
    edge_at = (1 - w) * (length - EDGE)

    def part(base, k):
        return at16(base + k * chunk, chunk)

    def raw_x(k):
        here = part(outer, k)
        return remote(own.at[here], near.at[here], 1, raw_x_sem.at[k], x_row, w)

    def raw_y(k):
        here = part(inner, k)
        return remote(own.at[here], near.at[here], 2, raw_y_sem.at[k], ahead, w)

    def hand(k):
        here = part(outer, k)
        return remote(near.at[here], far.at[here], 3, far_sem.at[k], behind, w)

    def sum_copy(here, k):
        return remote(made.at[here], given.at[here], 4, given_sem.at[k], x_row, w)

    def edge_copy(j):
        src = own if j == 0 else near
        return remote(
            src.at[at16(edge_at, EDGE)], edges.at[j], 5, edge_sem.at[j], r, other_w
        )

    def span(base, k):
        if isinstance(k, int) and k == 0:
            return base + EDGE, chunk - 2 * EDGE
        return base + k * chunk - EDGE, chunk

    side_at = half - EDGE
    key_copy = remote(
        right_hbm.at[0], keys.at[pl.ds(0, length)], 0, key_sem.at[0], r, other_w
    )

    def dots(value, tap):
        return [
            jnp.dot(value, weight[tap, b], preferred_element_type=jnp.float32) for b in range(3)
        ]

    def put(ref, base, k, values):
        for b in range(3):
            ref[b, at16(EDGE + base + k * chunk, chunk), :] = values[b]

    def add(ref, base, k, values):
        for b in range(3):
            here = at16(EDGE + base + k * chunk, chunk)
            ref[b, here, :] = ref[b, here, :] + values[b]

    def shifted(ref, start, n):
        before = ref[0, pl.ds(pl.multiple_of(start + EDGE - 8, 8), n + 8), :]
        after = ref[2, at16(start + EDGE, n + 8), :]
        return (
            pltpu.roll(before, 1, 0)[8:, :]
            + ref[1, at16(start + EDGE, n), :]
            + pltpu.roll(after, n + 7, 0)[:n, :]
        )

    def emit(start, n, with_given):
        here = at16(start, n)
        total = shifted(sums, start, n)
        if with_given:
            total = total + given[here, :].astype(jnp.float32)
        out_ref[0, here, :] = total.astype(bf16)

    def give(start, n, k):
        here = at16(start, n)
        made[here, :] = shifted(parts, start, n).astype(bf16)
        sum_copy(here, k).start()

    def loop(body):
        body(0)
        lax.fori_loop(1, n_chunks, lambda k, _: (body(k), 0)[1], 0)

    def prepare(k, _):
        put(sums, outer, k, dots(own[part(outer, k), :], 1))
        value = own[part(inner, k), :]
        put(sums, inner, k, dots(value, 1))
        put(parts, inner, k, dots(value, far_tap))
        return 0

    def take_x(k):
        raw_x(k).wait_recv()

        @pl.when(to_behind)
        def _():
            hand(k).start()

        add(sums, outer, k, dots(near[part(outer, k), :], x_tap))

    def take_y(k):
        @pl.when(to_behind)
        def _():
            raw_y(k).wait_recv()

            @pl.when(k == (1 - w) * (n_chunks - 1))
            def _():
                edge_copy(1).start()

            add(parts, inner, k, dots(near[part(inner, k), :], x_tap))

        give(*span(inner, k), k)

    def take_far(k):
        @pl.when(to_ahead)
        def _():
            hand(k).wait_recv()
            add(sums, outer, k, dots(far[part(outer, k), :], far_tap))

        emit(*span(outer, k), False)

    def take_given(k):
        start, n = span(inner, k)
        sum_copy(at16(start, n), k).wait_recv()
        emit(start, n, True)

    def clear():
        zeros = jnp.zeros((EDGE, chans), jnp.float32)
        sums[0, pl.ds(0, EDGE), :] = zeros
        sums[2, pl.ds(EDGE + length, EDGE), :] = zeros
        for b in range(3):
            for k in range(2):
                parts[b, at16(EDGE + half - (2 - k) * EDGE + 2 * w * EDGE, EDGE), :] = zeros

    def rim():
        edge_copy(0).wait_recv()
        tap_col = 2 - 2 * w
        ours = jnp.dot(edges[0], weight[1, tap_col], preferred_element_type=jnp.float32)
        theirs = jnp.dot(edges[0], weight[far_tap, tap_col], preferred_element_type=jnp.float32)
        here = at16(other_w * (EDGE + length), EDGE)
        sums[tap_col, here, :] = ours
        parts[tap_col, here, :] = theirs

        @pl.when(to_behind)
        def _():
            edge_copy(1).wait_recv()
            parts[tap_col, here, :] = theirs + jnp.dot(
                edges[1], weight[x_tap, tap_col], preferred_element_type=jnp.float32
            )

        give(side_at, 2 * EDGE, n_chunks)
        give(edge_at, EDGE, n_chunks + 1)

    held = (held_max, held_total, held_position, held_acc)
    per_tile = size // chunk

    def send_tile(tile, is_inner):
        for k in range(tile * per_tile, (tile + 1) * per_tile):
            if not is_inner:
                raw_x(k % n_chunks).start()
            else:

                @pl.when(to_ahead)
                def _():
                    raw_y(k % n_chunks).start()

    def mixed(lag):
        take_y(0)

        def step(k, _):
            @pl.when(k < n_chunks)
            def _():
                take_y(k)

            @pl.when(k >= lag)
            def _():
                take_x(k - lag)

            return 0

        lax.fori_loop(1, n_chunks + lag, step, 0)

    @pl.when(w == 0)
    def _():
        load_weight.start()
        inner_tiles = list(range(n_tiles // 2, n_tiles))
        for at, tile in enumerate([0, *inner_tiles, *range(1, n_tiles // 2)]):
            if at < 2:
                loaded(at)
            attend_all(left, keys, scores, own, disp_ref, tile, size)
            if at == 0:
                all_in()
                key_copy.start()
            send_tile(tile, tile >= n_tiles // 2)
        edge_copy(0).start()
        load_weight.wait()
        clear()
        lax.fori_loop(0, n_chunks, prepare, 0)
        mixed(1)

    @pl.when(w == 1)
    def _():
        load_weight.start()
        for tile in range(n_tiles):
            if tile < 2:
                loaded(tile)
            attend_own(left, keys, scores, held, tile, n_tiles, size)
        load_weight.wait()
        clear()
        all_in()
        key_copy.wait_recv()
        for tile in range(n_tiles):
            attend_rest(left, keys, scores, held, own, disp_ref, tile, n_tiles, size)
            if tile == 0:
                edge_copy(0).start()
            send_tile(tile, tile < n_tiles // 2)
        lax.fori_loop(0, n_chunks, prepare, 0)
        mixed(1)

    rim()

    def last(k):
        take_far(k)
        take_given(k)

    loop(last)
    sum_copy(at16(edge_at, EDGE), n_chunks + 1).wait_recv()
    emit(w * (length - EDGE), EDGE, False)
    emit(edge_at, EDGE, True)
    sum_copy(at16(side_at, 2 * EDGE), n_chunks).wait_recv()
    emit(side_at, 2 * EDGE, True)

    def sent(ref, n, which):
        remote(ref.at[pl.ds(0, n)], ref.at[pl.ds(0, n)], which, key_sem.at[0], x_row, w).wait_send()

    @pl.when(w == 0)
    def _():
        key_copy.wait_send()

    sent(own, half, 1)
    sent(made, half + EDGE, 4)
    sent(edges, 1, 5)

    @pl.when(to_ahead)
    def _():
        sent(own, half, 2)

    @pl.when(to_behind)
    def _():
        sent(near, half, 3)
        sent(edges, 1, 5)


def hand_on(disp_in, out_in, disp_ref, out_ref, sem):
    copies = [
        pltpu.make_async_copy(out_in, out_ref, sem.at[0]),
        pltpu.make_async_copy(disp_in, disp_ref, sem.at[1]),
    ]
    for copy in copies:
        copy.start()
    for copy in copies:
        copy.wait()


def fused(n_rows, left_feat, right_feat, refine_weight):
    _, length, chans = left_feat.shape
    half = length // 2
    size = math.gcd(half, 256)
    chunk = math.gcd(size, CHUNK)
    n_chunks = half // chunk
    bf16, f32 = jnp.bfloat16, jnp.float32
    dma = pltpu.SemaphoreType.DMA
    rows = pltpu.VMEM((length, chans), bf16)
    found = pl.pallas_call(
        functools.partial(kernel, n_rows, size, chunk),
        out_shape=(pltpu.VMEM((1, length), f32), pltpu.VMEM((1, length, chans), bf16)),
        in_specs=[pl.BlockSpec(memory_space=pltpu.HBM)] * 3,
        out_specs=[pl.BlockSpec(memory_space=pltpu.VMEM)] * 2,
        scratch_shapes=[
            rows,
            pltpu.VMEM((2 * length, chans), bf16),
            pltpu.VMEM((3, 3, chans, chans), bf16),
            pltpu.VMEM((size, 2 * length), f32),
            rows,
            rows,
            rows,
            rows,
            rows,
            pltpu.VMEM((2, EDGE, chans), bf16),
            pltpu.VMEM((3, length + 2 * EDGE, chans), f32),
            pltpu.VMEM((3, length + 2 * EDGE, chans), f32),
            pltpu.VMEM((length, LANES), f32),
            pltpu.VMEM((length, LANES), f32),
            pltpu.VMEM((length, LANES), f32),
            pltpu.VMEM((length, chans), f32),
            dma((5,)),
            dma((6,)),
            dma((1,)),
            dma((n_chunks,)),
            dma((n_chunks,)),
            dma((n_chunks,)),
            dma((n_chunks + 2,)),
            dma((2,)),
        ],
        compiler_params=pltpu.CompilerParams(
            collective_id=0, has_side_effects=True, vmem_limit_bytes=VMEM_LIMIT
        ),
    )(*(pltpu.with_memory_space_constraint(x, pltpu.HBM) for x in (left_feat, right_feat, refine_weight)))
    return pl.pallas_call(
        hand_on,
        out_shape=(
            jax.ShapeDtypeStruct((1, length), f32),
            jax.ShapeDtypeStruct((1, length, chans), bf16),
        ),
        in_specs=[pl.BlockSpec(memory_space=pltpu.VMEM)] * 2,
        out_specs=[pl.BlockSpec(memory_space=pltpu.HBM)] * 2,
        scratch_shapes=[dma((2,))],
        compiler_params=pltpu.CompilerParams(vmem_limit_bytes=VMEM_LIMIT),
    )(*found)


def solution(mesh):
    n_rows, n_width = mesh.shape["rows"], mesh.shape["width"]

    def local(left_feat, right_feat, refine_weight):
        rows_here, length, chans = left_feat.shape
        fits = n_rows % 2 == 0 and n_width == 2 and rows_here == 1
        if fits and length % (2 * CHUNK) == 0 and chans % LANES == 0:
            return fused(n_rows, left_feat, right_feat, refine_weight)
        return body(left_feat, right_feat, refine_weight)

    placed = (P("rows", "width", None), P("rows", "width", None), P())
    return jax.shard_map(
        local,
        mesh=mesh,
        in_specs=placed,
        out_specs=(P("rows", "width"), P("rows", "width", None)),
        check_vma=False,
    )
```
